32 devices in a mesh: wide: 8 (over z, x), narrow: 4 (over y, core).
Axes of the slice: x: 2, y: 2, z: 4, core: 2. Of those that a mesh axis runs over, the one named last changes fastest.
Arguments:
- tokens: bfloat16 [16384, 768], P('wide'), may hold values from -6 to 6
- cotangent: bfloat16 [16384, 768], P(('wide', 'narrow')), may hold values from -6 to 6
- lengths: int32 [8, 8], P('wide'), may hold values from 1 to 576, 2048 in all within a row
- routes: int32 [16384, 2], P(('wide', 'narrow')), may hold values from 0 to 7, as said below
- capacity_slots: int32 [16384, 2], P(('wide', 'narrow')), may hold values from 0 to 135, as said below
- first_gain: float32 [768], replicated, may hold values from 0.5 to 1.5
- second_gain: float32 [768], replicated, may hold values from 0.5 to 1.5
- query_weight: bfloat16 [768, 768], P(None, 'narrow'), may hold values from -0.21875 to 0.21875
- key_weight: bfloat16 [768, 768], P(None, 'narrow'), may hold values from -0.21875 to 0.21875
- value_weight: bfloat16 [768, 768], P(None, 'narrow'), may hold values from -0.21875 to 0.21875
- out_weight: bfloat16 [768, 768], P('narrow'), may hold values from -2 to 2
- router_weight: bfloat16 [768, 8], replicated, may hold values from -0.15625 to 0.15625
- expert_in: bfloat16 [8, 768, 3072], P('wide', None, 'narrow'), may hold values from -0.21875 to 0.21875
- expert_out: bfloat16 [8, 3072, 768], P('wide', 'narrow'), may hold values from -0.75 to 0.75
Outputs:
- block_output: bfloat16 [16384, 768], P(('wide', 'narrow'))
- token_grad: float32 [16384, 768], P(('wide', 'narrow'))
- first_gain_grad: float32 [768], P('narrow')
- second_gain_grad: float32 [768], P('narrow')
- query_weight_grad: float32 [768, 768], P(None, 'narrow')
- key_weight_grad: float32 [768, 768], P(None, 'narrow')
- value_weight_grad: float32 [768, 768], P(None, 'narrow')
- out_weight_grad: float32 [768, 768], P('narrow')
- router_weight_grad: float32 [768, 8], P('narrow')
- expert_in_grad: float32 [8, 768, 3072], P('wide', None, 'narrow')
- expert_out_grad: float32 [8, 3072, 768], P('wide', 'narrow')
The draws below stay inside these ranges and needn't reach their ends.
Inputs may be any that keep to these rules, and one draw needn't show every extreme that they name: `routes`: each row names two different experts. Within each device's block of 512 rows, the pairs that name one expert are ranked, all first choices before all second choices and in a fixed priority order among each; capacity_slots holds that rank, or 135 where the rank is 135 or more (a dropped pair). Kept pairs of one expert in one block have distinct slots.
All inputs are finite; a program needn't handle non-finite values.
Results may differ from the reference program's by a relative error of at most 0.019.
Values may be sent and summed in bfloat16 or wider, within the bound.
A program may use at most 192 MiB of HBM per device.

```python
import math
import jax
import jax.numpy as jnp
import numpy as np
from jax import lax

D = 768
HEADS = 12
HDIM = 64
FF = 3072
TOK_DEV = 512
MAXLEN = 576
QBLK = 512
GROUP = 2048
TOKENS = 16384
IMGS = 8
EXPERTS = 8
CAP = 135
N_WIDE = 8
N_NARROW = 4


def route_tables(key):
    base = jax.random.fold_in(key, 11)
    raw_scores = jax.random.randint(jax.random.fold_in(base, 1), (TOKENS, EXPERTS), 0, 65536)
    preference = jax.random.randint(jax.random.fold_in(base, 2), (EXPERTS,), 0, 32768)
    scores = (raw_scores + preference[None, :]) * EXPERTS + jnp.arange(EXPERTS, dtype=jnp.int32)[None, :]
    unused_top, chosen = lax.top_k(scores, 2)
    favourite = jax.random.randint(jax.random.fold_in(base, 3), (), 0, EXPERTS)
    forced = jax.random.randint(jax.random.fold_in(base, 4), (TOKENS,), 0, 4) == 0
    first_choice = jnp.where(forced, favourite, chosen[:, 0])
    second_choice = jnp.where(forced, jnp.where(chosen[:, 0] == favourite, chosen[:, 1], chosen[:, 0]), chosen[:, 1])
    routes_all = jnp.stack([first_choice, second_choice], axis=1).astype(jnp.int32)
    block_count = TOKENS // TOK_DEV
    block_routes = routes_all.reshape(block_count, TOK_DEV, 2)
    block_keys = jax.random.split(jax.random.fold_in(base, 5), block_count)

    def block_slots(block_key, route_block):
        priority = jax.random.permutation(block_key, TOK_DEV).astype(jnp.int32)
        order = jnp.stack([priority, priority + TOK_DEV], axis=1).reshape(-1)
        sorted_expert = jnp.zeros((2 * TOK_DEV,), jnp.int32).at[order].set(route_block.reshape(-1))
        onehot = (sorted_expert[:, None] == jnp.arange(EXPERTS, dtype=jnp.int32)[None, :]).astype(jnp.int32)
        before = jnp.cumsum(onehot, axis=0) - onehot
        rank_sorted = jnp.sum(before * onehot, axis=1)
        ranks = rank_sorted[order].reshape(TOK_DEV, 2)
        return jnp.minimum(ranks, CAP).astype(jnp.int32)
    slot_table = jax.vmap(block_slots)(block_keys, block_routes).reshape(TOKENS, 2)
    return (routes_all, slot_table)


def draw_routes(key, part):
    return route_tables(key)[0]


def draw_capacity_slots(key, part):
    return route_tables(key)[1]


def block_levels(key, shape, cuts, smallest, largest):
    level, own = 1.0, jax.random.fold_in(key, 6)
    for axis_at, parts in cuts:
        draws = jnp.exp(jax.random.uniform(jax.random.fold_in(own, axis_at), (parts,), jnp.float32, smallest / len(cuts), largest / len(cuts)))
        level = level * jnp.repeat(draws, shape[axis_at] // parts).reshape([-1 if axis == axis_at else 1 for axis in range(len(shape))])
    return level


def split_up(number_of, total, bound, lean):
    weights = [(1 << 20) // math.isqrt(standing ** lean) + 1 for standing in range(2, number_of + 1)]
    rest, holding = total - bound - (number_of - 1), [1] * (number_of - 1)
    while rest > 0:
        candidates = [i for i in range(number_of - 1) if holding[i] < bound]
        pool, budget = sum([weights[i] for i in candidates]), rest
        for i in candidates:
            extra = min(bound - holding[i], max(1, budget * weights[i] // pool), rest)
            holding[i] = holding[i] + extra
            rest = rest - extra
    return np.array([bound] + holding)


def uneven(stream_key, count, total, bound, slope):
    if count == 2:
        one = jax.random.randint(stream_key, (), max(1, total - bound), min(bound, total - 1) + 1)
        return jnp.stack([one, total - one])
    sizes = jnp.asarray(split_up(count, total, bound, slope), jnp.int32)
    twos = (count - 1) // 2
    source_of, sink = sizes[1:1 + 2 * twos:2], sizes[2:2 + 2 * twos:2]
    slack = jnp.minimum(source_of - 1, bound - sink)
    moved = jax.random.randint(jax.random.fold_in(stream_key, 1), (twos,), 0, 1 << 20) % (slack + 1)
    sizes = sizes.at[1:1 + 2 * twos:2].set(source_of - moved).at[2:2 + 2 * twos:2].set(sink + moved)
    return sizes[jax.random.permutation(jax.random.fold_in(stream_key, 2), count)]


def scatter_about(stream_key, extent, scale, reach, cuts=(), kind=jnp.bfloat16):
    entries = scale * jax.random.normal(stream_key, extent, jnp.float32)
    if cuts:
        entries = entries * block_levels(stream_key, extent, cuts, -0.22, 0.18)
    return jnp.clip(entries, -reach, reach).astype(kind)


def setup_inputs(seed: int = 0) -> dict:
    arg_keys = jax.random.split(jax.random.key(seed), 15)
    tokens = scatter_about(arg_keys[0], (TOKENS, D), 1.0, 6.0, ((0, 8),))
    cotangent = scatter_about(arg_keys[1], (TOKENS, D), 1.0, 6.0, ((0, 32),))
    lengths = jax.vmap(lambda own: uneven(own, IMGS, GROUP, MAXLEN, 2))(jax.random.split(arg_keys[2], N_WIDE)).reshape((N_WIDE, IMGS)).astype(jnp.int32)
    routes = draw_routes(jax.random.fold_in(arg_keys[14], 71), 0)
    capacity_slots = draw_capacity_slots(jax.random.fold_in(arg_keys[14], 71), 0)
    first_gain = jnp.clip(1.0 + 0.1 * jax.random.normal(arg_keys[5], (D,), jnp.float32), 0.5, 1.5)
    second_gain = jnp.clip(1.0 + 0.1 * jax.random.normal(arg_keys[6], (D,), jnp.float32), 0.5, 1.5)
    query_weight = scatter_about(arg_keys[7], (D, D), D ** -0.5, 0.21875, ((1, 4),))
    key_weight = scatter_about(arg_keys[8], (D, D), D ** -0.5, 0.21875, ((1, 4),))
    value_weight = scatter_about(arg_keys[9], (D, D), D ** -0.5, 0.21875, ((1, 4),))
    out_weight = scatter_about(arg_keys[10], (D, D), (max(D // 96, 1)) ** -0.5, 2.0, ((0, 4),))
    router_weight = scatter_about(arg_keys[11], (D, EXPERTS), (2 * D) ** -0.5, 0.15625)
    expert_in = scatter_about(arg_keys[12], (EXPERTS, D, FF), D ** -0.5, 0.21875, ((0, 8), (2, 4)))
    expert_out = scatter_about(arg_keys[13], (EXPERTS, FF, D), (max(3 * FF // (2 * EXPERTS * EXPERTS), 1)) ** -0.5, 0.75, ((0, 8), (1, 4)))
    return {"tokens": tokens, "cotangent": cotangent, "lengths": lengths, "routes": routes, "capacity_slots": capacity_slots, "first_gain": first_gain, "second_gain": second_gain, "query_weight": query_weight, "key_weight": key_weight, "value_weight": value_weight, "out_weight": out_weight, "router_weight": router_weight, "expert_in": expert_in, "expert_out": expert_out}


@jax.custom_vjp
def low(v):
    return lax.optimization_barrier(v.astype(jnp.bfloat16)).astype(jnp.float32)

@jax.custom_vjp
def low_back(v):
    return v

def low_keep(v):
    return (low(v), None)

def low_pass(kept, grad):
    return (grad,)

def back_keep(v):
    return (v, None)

def back_low(kept, grad):
    return (low(grad),)
low.defvjp(low_keep, low_pass)
low_back.defvjp(back_keep, back_low)
norm_eps = 1e-06
neg_large = -1e+30

def matmul(left, right):
    return jnp.dot(left, right, precision=lax.Precision.HIGHEST, preferred_element_type=jnp.float32)

def layer_norm(values, gain):
    mean_row = lax.optimization_barrier(jnp.mean(values, axis=-1, keepdims=True))
    centred = values - mean_row
    variance = lax.optimization_barrier(jnp.mean(centred * centred, axis=-1, keepdims=True))
    return centred * lax.rsqrt(variance + norm_eps) * gain

def softmax_rows(values):
    row_top = lax.optimization_barrier(jnp.max(values, axis=-1, keepdims=True))
    exponent = jnp.exp(values - row_top)
    return exponent / lax.optimization_barrier(jnp.sum(exponent, axis=-1, keepdims=True))

def attend_group(group_args):
    queries, keys_all, values_all, segment = group_args
    score_scale = 1.0 / math.sqrt(HDIM)
    window = QBLK + 2 * MAXLEN

    def one_block(query_begin):
        key_begin = jnp.clip(query_begin - MAXLEN, 0, GROUP - window)
        query_block = lax.dynamic_slice_in_dim(queries, query_begin, QBLK, 0)
        key_block = lax.dynamic_slice_in_dim(keys_all, key_begin, window, 0)
        value_block = lax.dynamic_slice_in_dim(values_all, key_begin, window, 0)
        same_image = lax.dynamic_slice_in_dim(segment, query_begin, QBLK, 0)[:, None] == lax.dynamic_slice_in_dim(segment, key_begin, window, 0)[None, :]
        scores = jnp.einsum('qhd,khd->hqk', query_block, key_block, precision=lax.Precision.HIGHEST) * score_scale
        scores = low_back(jnp.where(same_image[None], scores, neg_large))
        probs = softmax_rows(scores)
        return jnp.einsum('hqk,khd->qhd', low(probs), value_block, precision=lax.Precision.HIGHEST)
    starts = jnp.arange(GROUP // QBLK, dtype=jnp.int32) * QBLK
    outputs = lax.map(jax.checkpoint(one_block), starts)
    return outputs.reshape(GROUP, HEADS, HDIM)

def run_expert(expert_args):
    slot_inputs, weight_in, weight_out = expert_args
    pre_act = low_back(matmul(slot_inputs, weight_in))
    act_low = low(jax.nn.gelu(pre_act, approximate=False))
    return low_back(low(matmul(act_low, weight_out)))

def reference(tokens, cotangent, lengths, routes, capacity_slots, first_gain, second_gain, query_weight, key_weight, value_weight, out_weight, router_weight, expert_in, expert_out):
    device_count = N_WIDE * N_NARROW
    image_ends = jnp.cumsum(lengths, axis=1)
    positions = jnp.arange(GROUP, dtype=jnp.int32)
    segment = lax.optimization_barrier(jnp.sum((positions[None, :, None] >= image_ends[:, None, :]).astype(jnp.int32), axis=2))
    kept = (capacity_slots < CAP).astype(jnp.float32)
    block_routes = routes.reshape(device_count, TOK_DEV, 2)
    block_slots = capacity_slots.reshape(device_count, TOK_DEV, 2)
    pick_slots = jnp.minimum(block_slots, CAP - 1)

    def make_table(route_block, slot_block):
        token_ids = jnp.broadcast_to(jnp.arange(TOK_DEV, dtype=jnp.int32)[:, None], (TOK_DEV, 2))
        filled = jnp.full((EXPERTS, CAP + 1), TOK_DEV, jnp.int32).at[route_block, slot_block].set(token_ids)
        return filled[:, :CAP]
    tables = jax.vmap(make_table)(block_routes, block_slots)
    expert_ids = jnp.arange(EXPERTS, dtype=jnp.int32)
    onehot = (routes[:, :, None] == expert_ids[None, None, :]).astype(jnp.float32)

    def forward(whole, gain_a, gain_b, weight_q, weight_k, weight_v, weight_o, weight_r, weight_in, weight_out):
        attn_in = low(layer_norm(whole, gain_a))

        def project(weight):
            return low_back(low(matmul(attn_in, weight))).reshape(N_WIDE, GROUP, HEADS, HDIM)
        attended = lax.map(attend_group, (project(weight_q), project(weight_k), project(weight_v), segment))
        attended = low_back(low(attended.reshape(TOKENS, D)))
        hidden_one = whole + low_back(matmul(attended, weight_o))
        moe_in = low(layer_norm(hidden_one, gain_b))
        router_probs = softmax_rows(low_back(matmul(moe_in, weight_r)))
        gate = lax.optimization_barrier(jnp.sum(onehot * router_probs[:, None, :], axis=2)) * kept
        padded = jnp.concatenate([moe_in.reshape(device_count, TOK_DEV, D), jnp.zeros((device_count, 1, D), jnp.float32)], axis=1)
        sent = jax.vmap(lambda source_rows, slot_table: source_rows[slot_table])(padded, tables)
        expert_rows = low_back(jnp.swapaxes(sent, 0, 1).reshape(EXPERTS, device_count * CAP, D))
        result = lax.map(jax.checkpoint(run_expert), (expert_rows, weight_in, weight_out))
        result = jnp.swapaxes(result.reshape(EXPERTS, device_count, CAP, D), 0, 1)
        picked = jax.vmap(lambda found, route_block, slot_block: found[route_block, slot_block])(result, block_routes, pick_slots)
        picked = picked.reshape(TOKENS, 2, D)
        return hidden_one + lax.optimization_barrier(jnp.sum(gate[:, :, None] * picked, axis=1))
    primals = (tokens.astype(jnp.float32), first_gain.astype(jnp.float32), second_gain.astype(jnp.float32), query_weight.astype(jnp.float32), key_weight.astype(jnp.float32), value_weight.astype(jnp.float32), out_weight.astype(jnp.float32), router_weight.astype(jnp.float32), expert_in.astype(jnp.float32), expert_out.astype(jnp.float32))
    output, pullback = jax.vjp(forward, *primals)
    grads = pullback(cotangent.astype(jnp.float32))
    return (output.astype(jnp.bfloat16), grads[0], grads[1], grads[2], grads[3], grads[4], grads[5], grads[6], grads[7], grads[8], grads[9])
```

```python
import functools
import math

import jax
import jax.numpy as jnp
from jax import lax
from jax.experimental import pallas as pl
from jax.experimental.pallas import tpu as pltpu
from jax.sharding import PartitionSpec as P

HDIM = 64
TILE = 256
BIG = 1e30
norm_eps = 1e-06
F32, BF16 = jnp.float32, jnp.bfloat16


def dot_nn(a, b):
    return lax.dot_general(a, b, (((1,), (0,)), ((), ())), preferred_element_type=F32)


def dot_nt(a, b):
    return lax.dot_general(a, b, (((1,), (1,)), ((), ())), preferred_element_type=F32)


def image_bounds(len_ref):
    ends = []
    total = jnp.int32(0)
    for image in range(len_ref.shape[1]):
        total = total + len_ref[0, image]
        ends.append(total)
    return [jnp.int32(0)] + ends[:-1], ends


def tile_range(starts, ends, tile):
    first, last = tile * TILE, tile * TILE + (TILE - 1)
    low, high = jnp.int32(0), jnp.int32(0)
    for begin, end in zip(starts, ends):
        low = jnp.where((begin <= first) & (first < end), begin, low)
        high = jnp.where((begin <= last) & (last < end), end, high)
    return low // TILE, (high + (TILE - 1)) // TILE


def head_mask(width, head, lanes):
    lane = lax.broadcasted_iota(jnp.int32, (1, lanes), 1)
    return ((lane >= head * HDIM) & (lane < (head + 1) * HDIM)) | (lane >= width)


def fwd_kernel(len_ref, tok_ref, gain_ref, wq_ref, wk_ref, wv_ref,
               attn_in_ref, att_ref, lse_ref, q_ref, kt_ref, kn_ref, vn_ref,
               kh_ref, vt_ref, s_ref):
    group, _ = tok_ref.shape
    width = wq_ref.shape[0]
    heads = width // HDIM
    lanes = q_ref.shape[0]
    tiles = group // TILE
    per_block = att_ref.shape[2] // TILE
    starts, ends = image_bounds(len_ref)

    def project(tile, _):
        rows = pl.ds(pl.multiple_of(tile * TILE, TILE), TILE)
        values = tok_ref[rows, :].astype(F32)
        centred = values - jnp.mean(values, axis=1, keepdims=True)
        variance = jnp.mean(centred * centred, axis=1, keepdims=True)
        normed = (centred * lax.rsqrt(variance + norm_eps) * gain_ref[...]).astype(BF16)
        attn_in_ref[rows, :] = normed
        q_ref[0:width, rows] = (dot_nt(wq_ref[...], normed).astype(BF16).astype(F32) * (1.0 / math.sqrt(HDIM))).astype(BF16)
        kt_ref[:, rows] = dot_nt(wk_ref[0:width, :], normed).astype(BF16)
        vt_ref[:, rows] = dot_nt(wv_ref[0:width, :], normed).astype(BF16)
        keys = dot_nt(normed, wk_ref[...]).astype(BF16).astype(F32)
        vn_ref[rows, :] = dot_nt(normed, wv_ref[...]).astype(BF16)
        place = tile * TILE + lax.broadcasted_iota(jnp.int32, (TILE, lanes), 0)
        lane = lax.broadcasted_iota(jnp.int32, (TILE, lanes), 1)
        here = tile * TILE + lax.broadcasted_iota(jnp.int32, (lanes - width, TILE), 1)
        row = lax.broadcasted_iota(jnp.int32, (lanes - width, TILE), 0)
        feature = jnp.zeros((lanes - width, TILE), F32)
        for image, (begin, end) in enumerate(zip(starts, ends)):
            keys = jnp.where((lane == width + image) & (place >= begin) & (place < end), 1.0, keys)
            feature = jnp.where((row == image) & ((here < begin) | (here >= end)), -BIG, feature)
        q_ref[width:lanes, rows] = feature.astype(BF16)
        kn_ref[rows, :] = keys.astype(BF16)
        for head in range(heads):
            kh_ref[head, rows, :] = jnp.where(head_mask(width, head, lanes), keys, 0.0).astype(BF16)
        return 0

    lax.fori_loop(0, tiles, project, 0)

    def attend(tile, _):
        columns = pl.ds(pl.multiple_of(tile * TILE, TILE), TILE)
        low, high = tile_range(starts, ends, tile)
        queries = q_ref[:, columns]

        def score(key_tile, tops):
            rows = pl.ds(pl.multiple_of(key_tile * TILE, TILE), TILE)
            result = []
            for head in range(heads):
                scores = dot_nn(kh_ref[head, rows, :], queries)
                s_ref[key_tile - low, head] = scores
                result.append(jnp.maximum(tops[head], jnp.max(scores, axis=0, keepdims=True)))
            return tuple(result)

        tops = lax.fori_loop(low, high, score, tuple(jnp.full((1, TILE), -3e38, F32) for _ in range(heads)))

        def gather(key_tile, carry):
            totals, parts = carry
            rows = pl.ds(pl.multiple_of(key_tile * TILE, TILE), TILE)
            new_totals, new_parts = [], []
            for head in range(heads):
                weight = jnp.exp(s_ref[key_tile - low, head] - tops[head])
                new_totals.append(totals[head] + jnp.sum(weight, axis=0, keepdims=True))
                new_parts.append(parts[head] + dot_nn(vt_ref[head * HDIM:(head + 1) * HDIM, rows], weight.astype(BF16)))
            return tuple(new_totals), tuple(new_parts)

        zero = tuple(jnp.zeros((1, TILE), F32) for _ in range(heads))
        zero_parts = tuple(jnp.zeros((HDIM, TILE), F32) for _ in range(heads))
        totals, parts = lax.fori_loop(low, high, gather, (zero, zero_parts))
        spot = pl.ds(pl.multiple_of(lax.rem(tile, per_block) * TILE, TILE), TILE)
        for head in range(heads):
            att_ref[tile // per_block, head * HDIM:(head + 1) * HDIM, spot] = (parts[head] / totals[head]).astype(BF16)
            lse_ref[head:head + 1, columns] = tops[head] + jnp.log(totals[head])
        return 0

    lax.fori_loop(0, tiles, attend, 0)


def bwd_kernel(len_ref, q_ref, kt_ref, kn_ref, vn_ref, lse_ref, att_ref, do_ref,
               out_ref, kh_ref, vh_ref, delta_ref, dq_ref, dk_ref, dv_ref):
    width, group = kt_ref.shape
    heads = width // HDIM
    lanes = kn_ref.shape[1]
    tiles = group // TILE
    per_block = do_ref.shape[2] // TILE
    starts, ends = image_bounds(len_ref)

    def prepare(tile, _):
        rows = pl.ds(pl.multiple_of(tile * TILE, TILE), TILE)
        spot = pl.ds(pl.multiple_of(lax.rem(tile, per_block) * TILE, TILE), TILE)
        keys, values = kn_ref[rows, :].astype(F32), vn_ref[rows, :].astype(F32)
        for head in range(heads):
            mask = head_mask(width, head, lanes)
            kh_ref[head, rows, :] = jnp.where(mask, keys, 0.0).astype(BF16)
            vh_ref[head, rows, :] = jnp.where(mask, values, 0.0).astype(BF16)[:, 0:width]
            part = slice(head * HDIM, (head + 1) * HDIM)
            delta_ref[head:head + 1, rows] = jnp.sum(
                do_ref[tile // per_block, part, spot].astype(F32) * att_ref[tile // per_block, part, spot].astype(F32),
                axis=0, keepdims=True)
        dq_ref[:, rows] = jnp.zeros((width, TILE), F32)
        return 0

    lax.fori_loop(0, tiles, prepare, 0)

    def key_step(key_tile, _):
        rows = pl.ds(pl.multiple_of(key_tile * TILE, TILE), TILE)
        low, high = tile_range(starts, ends, key_tile)
        dk_ref[...] = jnp.zeros_like(dk_ref)
        dv_ref[...] = jnp.zeros_like(dv_ref)

        def query_step(tile, _):
            columns = pl.ds(pl.multiple_of(tile * TILE, TILE), TILE)
            spot = pl.ds(pl.multiple_of(lax.rem(tile, per_block) * TILE, TILE), TILE)
            queries = q_ref[:, columns]
            grads = do_ref[tile // per_block, :, spot]
            for head in range(heads):
                part = slice(head * HDIM, (head + 1) * HDIM)
                scores = dot_nn(kh_ref[head, rows, :], queries)
                probs = jnp.exp(scores - lse_ref[head:head + 1, columns])
                grad_weights = dot_nn(vh_ref[head, rows, :], grads)
                grad_scores = (probs * (grad_weights - delta_ref[head:head + 1, columns])).astype(BF16)
                dv_ref[part, :] += dot_nt(grads[part, :], probs.astype(BF16))
                dk_ref[part, :] += dot_nt(queries[part, :], grad_scores)
                dq_ref[part, columns] += dot_nn(kt_ref[part, rows], grad_scores)
            return 0

        lax.fori_loop(low, high, query_step, 0)
        out_ref[width:2 * width, rows] = dk_ref[...].astype(BF16)
        out_ref[2 * width:3 * width, rows] = dv_ref[...].astype(BF16)
        return 0

    lax.fori_loop(0, tiles, key_step, 0)
    out_ref[0:width, :] = (dq_ref[...] * (1.0 / math.sqrt(HDIM))).astype(BF16)


VM = pl.BlockSpec(memory_space=pltpu.VMEM)
SM = pl.BlockSpec(memory_space=pltpu.SMEM)
LIMIT = 60 * 2**20


def attn_fwd(lengths, tokens, gain, wq, wk, wv, blocks):
    group, model = tokens.shape
    width = wq.shape[0]
    lanes = wk.shape[0]
    heads = width // HDIM
    tiles = group // TILE
    S = jax.ShapeDtypeStruct
    return pl.pallas_call(
        fwd_kernel,
        out_shape=(S((group, model), BF16), S((blocks, width, group // blocks), BF16), S((8, group), F32),
                   S((lanes, group), BF16), S((width, group), BF16), S((group, lanes), BF16), S((group, lanes), BF16)),
        in_specs=[SM] + [VM] * 5, out_specs=(VM,) * 7,
        scratch_shapes=[pltpu.VMEM((heads, group, lanes), BF16), pltpu.VMEM((width, group), BF16),
                        pltpu.VMEM((tiles, heads, TILE, TILE), F32)],
        compiler_params=pltpu.CompilerParams(vmem_limit_bytes=LIMIT),
        cost_estimate=pl.CostEstimate(flops=8 * 10**9, bytes_accessed=10**7, transcendentals=4 * 10**6),
        name="attend_forward",
    )(lengths, tokens, gain, wq, wk, wv)


def attn_bwd(lengths, q, kt, kn, vn, lse, att, do):
    width, group = kt.shape
    lanes = kn.shape[1]
    heads = width // HDIM
    S = jax.ShapeDtypeStruct
    return pl.pallas_call(
        bwd_kernel,
        out_shape=S((3 * width, group), BF16),
        in_specs=[SM] + [VM] * 7, out_specs=VM,
        scratch_shapes=[pltpu.VMEM((heads, group, lanes), BF16), pltpu.VMEM((heads, group, width), BF16),
                        pltpu.VMEM((8, group), F32), pltpu.VMEM((width, group), F32),
                        pltpu.VMEM((width, TILE), F32), pltpu.VMEM((width, TILE), F32)],
        compiler_params=pltpu.CompilerParams(vmem_limit_bytes=LIMIT),
        cost_estimate=pl.CostEstimate(flops=16 * 10**9, bytes_accessed=10**7, transcendentals=4 * 10**6),
        name="attend_backward",
    )(lengths, q, kt, kn, vn, lse, att, do)


def matmul(left, right):
    return jnp.dot(left, right, preferred_element_type=F32)


def inner_rows(left, right):
    return lax.dot_general(left, right, (((0,), (0,)), ((), ())), preferred_element_type=F32)


def times_transposed(left, right):
    return lax.dot_general(left, right, (((1,), (1,)), ((), ())), preferred_element_type=F32)


def norm_rows(values):
    mean_row = jnp.mean(values, axis=-1, keepdims=True)
    centred = values - mean_row
    variance = jnp.mean(centred * centred, axis=-1, keepdims=True)
    root_inv = lax.rsqrt(variance + norm_eps)
    return (centred * root_inv, root_inv)


def norm_back(grad_scaled, normed, root_inv):
    first_mean = jnp.mean(grad_scaled, axis=-1, keepdims=True)
    second_mean = jnp.mean(grad_scaled * normed, axis=-1, keepdims=True)
    return root_inv * (grad_scaled - first_mean - normed * second_mean)


def gelu_parts(pre_act):
    normal_cdf = 0.5 * (1.0 + lax.erf(pre_act * 0.7071067811865476))
    density = jnp.exp(-0.5 * pre_act * pre_act) * 0.3989422804014327
    return (pre_act * normal_cdf, normal_cdf + pre_act * density)


def flip(value, bit):
    size = lax.axis_size("narrow")
    return lax.ppermute(value, "narrow", [(i, i ^ bit) for i in range(size)])


def swap_wide(rows, experts):
    shape = rows.shape
    return lax.all_to_all(
        rows.reshape(experts, -1, shape[1]), "wide", split_axis=0, concat_axis=0, tiled=True
    ).reshape(shape)


def swap_narrow(blocks):
    return lax.all_to_all(blocks, "narrow", split_axis=0, concat_axis=0, tiled=True)


def local(
    tokens,
    cotangent,
    lengths,
    routes,
    capacity_slots,
    first_gain,
    second_gain,
    query_weight,
    key_weight,
    value_weight,
    out_weight,
    router_weight,
    expert_in,
    expert_out,
):
    experts = lax.axis_size("wide")
    narrow = lax.axis_size("narrow")
    own_expert = lax.axis_index("wide")
    own_block = lax.axis_index("narrow")
    block_rows, model = cotangent.shape
    capacity = (42 * block_rows + 20 * experts - 1) // (20 * experts)
    slots = -(-capacity // 8) * 8
    width = query_weight.shape[1]

    in_here, out_here = expert_in[0], expert_out[0]
    out_there = flip(out_here, 2)
    in_there = flip(in_here, 2)
    out_parts = [out_here, flip(out_here, 1), out_there, flip(out_there, 1)]
    in_parts = [in_here, flip(in_here, 1), in_there, flip(in_there, 1)]
    out_full = lax.all_gather(out_weight, "narrow", axis=0, tiled=True)

    place = jnp.where(capacity_slots < capacity, routes * slots + capacity_slots, experts * slots)
    slot_ids = jnp.arange(experts * slots, dtype=jnp.int32)
    select = (
        (place[:, 0:1] == slot_ids[None, :]) | (place[:, 1:2] == slot_ids[None, :])
    ).astype(BF16)
    cot_rows = swap_wide(inner_rows(select, cotangent).astype(BF16), experts)

    query_t, key_t, value_t = query_weight.T, key_weight.T, value_weight.T
    lanes = -(-(width + lengths.shape[1]) // 128) * 128
    pad = ((0, lanes - width), (0, 0))
    attn_in, att, lse, q_keep, kt_keep, kn_keep, vn_keep = attn_fwd(
        lengths, tokens, first_gain[None], query_t, jnp.pad(key_t, pad), jnp.pad(value_t, pad), narrow
    )
    att_own = swap_narrow(att).reshape(narrow * width, block_rows)
    own_tokens = lax.dynamic_slice_in_dim(tokens, own_block * block_rows, block_rows, 0).astype(F32)
    hidden_one = own_tokens + inner_rows(att_own, out_full)
    normed_two, root_two = norm_rows(hidden_one)
    moe_in = (normed_two * second_gain).astype(BF16)
    rows = swap_wide(inner_rows(select, moe_in).astype(BF16), experts)

    logits = matmul(rows, router_weight)
    logit_exp = jnp.exp(logits - jnp.max(logits, axis=1, keepdims=True))
    probs = logit_exp / jnp.sum(logit_exp, axis=1, keepdims=True)
    mine = (jnp.arange(experts, dtype=jnp.int32) == own_expert).astype(F32)[None, :]
    gate = jnp.sum(probs * mine, axis=1, keepdims=True)
    grad_gate = jnp.zeros_like(gate)
    act_parts, pre_grads = [], []
    for w_in, w_out in zip(in_parts, out_parts):
        back = times_transposed(cot_rows, w_out).astype(BF16)
        activated, slope = gelu_parts(matmul(rows, w_in))
        act_low = activated.astype(BF16)
        act_parts.append(act_low)
        grad_gate = grad_gate + jnp.sum(act_low.astype(F32) * back.astype(F32), axis=1, keepdims=True)
        pre_grads.append((gate * back.astype(F32) * slope).astype(BF16))
    grad_logits = (grad_gate * probs * (mine - gate)).astype(BF16)
    grad_sum = times_transposed(grad_logits, router_weight)
    for pre_grad, w_in in zip(pre_grads, in_parts):
        grad_sum = grad_sum + times_transposed(pre_grad, w_in)
    grad_home = swap_wide(grad_sum.astype(BF16), experts)
    result = sum(matmul(act, w_out) for act, w_out in zip(act_parts, out_parts))
    result_home = swap_wide((gate * result).astype(BF16), experts)
    grad_result = (gate * cot_rows.astype(F32)).astype(BF16)
    router_part = inner_rows(rows, grad_logits)
    out_grads = [inner_rows(act, grad_result) for act in act_parts]
    in_grads = [inner_rows(rows, pre_grad) for pre_grad in pre_grads]

    def sum_narrow(parts):
        one, three = flip(parts[1].astype(BF16), 1), flip(parts[3].astype(BF16), 1)
        keep = parts[0] + one.astype(F32)
        send = (parts[2] + three.astype(F32)).astype(BF16)
        return keep + flip(send, 2).astype(F32)

    out_grad, in_grad = sum_narrow(out_grads)[None], sum_narrow(in_grads)[None]

    grad_moe_in = matmul(select, grad_home)
    mixed = hidden_one + matmul(select, result_home)
    block_output = mixed.astype(BF16)
    second_part = jnp.sum(grad_moe_in * normed_two, axis=0)
    grad_hidden = cotangent.astype(F32) + norm_back(grad_moe_in * second_gain, normed_two, root_two)
    grad_branch = grad_hidden.astype(BF16)
    grad_att = times_transposed(out_full, grad_branch).astype(BF16)
    grad_heads = swap_narrow(grad_att.reshape(narrow, width, block_rows))
    out_part = matmul(att_own, grad_branch)
    out_weight_grad = lax.psum(
        lax.psum_scatter(out_part, "narrow", scatter_dimension=0, tiled=True), "wide"
    )
    small = lax.psum(
        jnp.concatenate([router_part, second_part[:, None]], axis=1), ("wide", "narrow")
    )

    grad_qkv = attn_bwd(lengths, q_keep, kt_keep, kn_keep, vn_keep, lse, att, grad_heads)
    qkv_t = jnp.concatenate([query_t, key_t, value_t], axis=0)
    grad_attn_in = inner_rows(grad_qkv, qkv_t).astype(BF16).reshape(narrow, block_rows, model)

    def block_of(bits):
        return lax.dynamic_index_in_dim(grad_attn_in, own_block ^ bits, 0, keepdims=False)

    grad_rows_att = sum_narrow([block_of(bits).astype(F32) for bits in range(4)])
    qkv_part = lax.dot_general(
        attn_in, grad_qkv, (((0,), (1,)), ((), ())), preferred_element_type=F32
    )
    first_part = jnp.sum(qkv_part * qkv_t.T.astype(F32), axis=1) / first_gain
    qkv_grad = lax.psum(qkv_part, "wide")
    first = lax.psum(first_part, ("wide", "narrow"))
    own_normed, own_root = norm_rows(own_tokens)
    token_grad = grad_hidden + norm_back(grad_rows_att * first_gain, own_normed, own_root)

    def own_share(value):
        size = value.shape[0] // narrow
        return lax.dynamic_slice_in_dim(value, own_block * size, size, 0)

    small = own_share(small)
    return (
        block_output,
        token_grad,
        own_share(first),
        small[:, experts],
        qkv_grad[:, 0:width],
        qkv_grad[:, width:2 * width],
        qkv_grad[:, 2 * width:3 * width],
        out_weight_grad,
        small[:, 0:experts],
        in_grad,
        out_grad,
    )


def solution(mesh):
    in_specs = (
        P("wide", None),
        P(("wide", "narrow"), None),
        P("wide", None),
        P(("wide", "narrow"), None),
        P(("wide", "narrow"), None),
        P(),
        P(),
        P(None, "narrow"),
        P(None, "narrow"),
        P(None, "narrow"),
        P("narrow", None),
        P(),
        P("wide", None, "narrow"),
        P("wide", "narrow", None),
    )
    out_specs = (
        P(("wide", "narrow"), None),
        P(("wide", "narrow"), None),
        P("narrow"),
        P("narrow"),
        P(None, "narrow"),
        P(None, "narrow"),
        P(None, "narrow"),
        P("narrow", None),
        P("narrow", None),
        P("wide", None, "narrow"),
        P("wide", "narrow", None),
    )
    return jax.shard_map(local, mesh=mesh, in_specs=in_specs, out_specs=out_specs, check_vma=False)
```

```python
import functools
import math

import jax
import jax.numpy as jnp
from jax import lax
from jax.experimental import pallas as pl
from jax.experimental.pallas import tpu as pltpu
from jax.sharding import PartitionSpec as P

HDIM = 64
TILE = 256
BIG = 1e30
norm_eps = 1e-06
F32, BF16 = jnp.float32, jnp.bfloat16


def dot_nn(a, b):
    return lax.dot_general(a, b, (((1,), (0,)), ((), ())), preferred_element_type=F32)


def dot_nt(a, b):
    return lax.dot_general(a, b, (((1,), (1,)), ((), ())), preferred_element_type=F32)


def image_bounds(len_ref):
    ends = []
    total = jnp.int32(0)
    for image in range(len_ref.shape[1]):
        total = total + len_ref[0, image]
        ends.append(total)
    return [jnp.int32(0)] + ends[:-1], ends


def tile_range(starts, ends, tile):
    first, last = tile * TILE, tile * TILE + (TILE - 1)
    low, high = jnp.int32(0), jnp.int32(0)
    for begin, end in zip(starts, ends):
        low = jnp.where((begin <= first) & (first < end), begin, low)
        high = jnp.where((begin <= last) & (last < end), end, high)
    return low // TILE, (high + (TILE - 1)) // TILE


def head_mask(width, head, lanes):
    lane = lax.broadcasted_iota(jnp.int32, (1, lanes), 1)
    return ((lane >= head * HDIM) & (lane < (head + 1) * HDIM)) | (lane >= width)


def fwd_kernel(len_ref, tok_ref, gain_ref, wq_ref, wk_ref, wv_ref,
               attn_in_ref, att_ref, lse_ref, q_ref, kt_ref, kn_ref, vn_ref,
               kh_ref, vt_ref, s_ref):
    group, _ = tok_ref.shape
    width = wq_ref.shape[0]
    heads = width // HDIM
    lanes = q_ref.shape[0]
    tiles = group // TILE
    per_block = att_ref.shape[2] // TILE
    starts, ends = image_bounds(len_ref)

    def project(tile, _):
        rows = pl.ds(pl.multiple_of(tile * TILE, TILE), TILE)
        values = tok_ref[rows, :].astype(F32)
        centred = values - jnp.mean(values, axis=1, keepdims=True)
        variance = jnp.mean(centred * centred, axis=1, keepdims=True)
        normed = (centred * lax.rsqrt(variance + norm_eps) * gain_ref[...]).astype(BF16)
        attn_in_ref[rows, :] = normed
        q_ref[0:width, rows] = (dot_nt(wq_ref[...], normed).astype(BF16).astype(F32) * (1.0 / math.sqrt(HDIM))).astype(BF16)
        kt_ref[:, rows] = dot_nt(wk_ref[0:width, :], normed).astype(BF16)
        vt_ref[:, rows] = dot_nt(wv_ref[0:width, :], normed).astype(BF16)
        keys = dot_nt(normed, wk_ref[...]).astype(BF16).astype(F32)
        vn_ref[rows, :] = dot_nt(normed, wv_ref[...]).astype(BF16)
        place = tile * TILE + lax.broadcasted_iota(jnp.int32, (TILE, lanes), 0)
        lane = lax.broadcasted_iota(jnp.int32, (TILE, lanes), 1)
        here = tile * TILE + lax.broadcasted_iota(jnp.int32, (lanes - width, TILE), 1)
        row = lax.broadcasted_iota(jnp.int32, (lanes - width, TILE), 0)
        feature = jnp.zeros((lanes - width, TILE), F32)
        for image, (begin, end) in enumerate(zip(starts, ends)):
            keys = jnp.where((lane == width + image) & (place >= begin) & (place < end), 1.0, keys)
            feature = jnp.where((row == image) & ((here < begin) | (here >= end)), -BIG, feature)
        q_ref[width:lanes, rows] = feature.astype(BF16)
        kn_ref[rows, :] = keys.astype(BF16)
        for head in range(heads):
            kh_ref[head, rows, :] = jnp.where(head_mask(width, head, lanes), keys, 0.0).astype(BF16)
        return 0

    lax.fori_loop(0, tiles, project, 0)

    def attend(tile, _):
        columns = pl.ds(pl.multiple_of(tile * TILE, TILE), TILE)
        low, high = tile_range(starts, ends, tile)
        queries = q_ref[:, columns]

        def score(key_tile, tops):
            rows = pl.ds(pl.multiple_of(key_tile * TILE, TILE), TILE)
            result = []
            for head in range(heads):
                scores = dot_nn(kh_ref[head, rows, :], queries)
                s_ref[key_tile - low, head] = scores
                result.append(jnp.maximum(tops[head], jnp.max(scores, axis=0, keepdims=True)))
            return tuple(result)

        tops = lax.fori_loop(low, high, score, tuple(jnp.full((1, TILE), -3e38, F32) for _ in range(heads)))

        def gather(key_tile, carry):
            totals, parts = carry
            rows = pl.ds(pl.multiple_of(key_tile * TILE, TILE), TILE)
            new_totals, new_parts = [], []
            for head in range(heads):
                weight = jnp.exp(s_ref[key_tile - low, head] - tops[head])
                new_totals.append(totals[head] + jnp.sum(weight, axis=0, keepdims=True))
                new_parts.append(parts[head] + dot_nn(vt_ref[head * HDIM:(head + 1) * HDIM, rows], weight.astype(BF16)))
            return tuple(new_totals), tuple(new_parts)

        zero = tuple(jnp.zeros((1, TILE), F32) for _ in range(heads))
        zero_parts = tuple(jnp.zeros((HDIM, TILE), F32) for _ in range(heads))
        totals, parts = lax.fori_loop(low, high, gather, (zero, zero_parts))
        spot = pl.ds(pl.multiple_of(lax.rem(tile, per_block) * TILE, TILE), TILE)
        for head in range(heads):
            att_ref[tile // per_block, head * HDIM:(head + 1) * HDIM, spot] = (parts[head] / totals[head]).astype(BF16)
            lse_ref[head:head + 1, columns] = tops[head] + jnp.log(totals[head])
        return 0

    lax.fori_loop(0, tiles, attend, 0)


def bwd_kernel(own_ref, len_ref, q_ref, kt_ref, kn_ref, vn_ref, lse_ref, att_ref, do_ref,
               out_ref, kh_ref, vh_ref, delta_ref, dq_ref, dk_ref, dv_ref):
    width, group = kt_ref.shape
    heads = width // HDIM
    lanes = kn_ref.shape[1]
    tiles = group // TILE
    per_block = do_ref.shape[2] // TILE
    starts, ends = image_bounds(len_ref)

    def prepare(tile, _):
        rows = pl.ds(pl.multiple_of(tile * TILE, TILE), TILE)
        spot = pl.ds(pl.multiple_of(lax.rem(tile, per_block) * TILE, TILE), TILE)
        keys, values = kn_ref[rows, :].astype(F32), vn_ref[rows, :].astype(F32)
        for head in range(heads):
            mask = head_mask(width, head, lanes)
            kh_ref[head, rows, :] = jnp.where(mask, keys, 0.0).astype(BF16)
            vh_ref[head, rows, :] = jnp.where(mask, values, 0.0).astype(BF16)[:, 0:width]
            part = slice(head * HDIM, (head + 1) * HDIM)
            delta_ref[head:head + 1, rows] = jnp.sum(
                do_ref[(tile // per_block) ^ own_ref[0], part, spot].astype(F32) * att_ref[tile // per_block, part, spot].astype(F32),
                axis=0, keepdims=True)
        dq_ref[:, rows] = jnp.zeros((width, TILE), F32)
        return 0

    lax.fori_loop(0, tiles, prepare, 0)

    def key_step(key_tile, _):
        rows = pl.ds(pl.multiple_of(key_tile * TILE, TILE), TILE)
        low, high = tile_range(starts, ends, key_tile)
        dk_ref[...] = jnp.zeros_like(dk_ref)
        dv_ref[...] = jnp.zeros_like(dv_ref)

        def query_step(tile, _):
            columns = pl.ds(pl.multiple_of(tile * TILE, TILE), TILE)
            spot = pl.ds(pl.multiple_of(lax.rem(tile, per_block) * TILE, TILE), TILE)
            queries = q_ref[:, columns]
            grads = do_ref[(tile // per_block) ^ own_ref[0], :, spot]
            for head in range(heads):
                part = slice(head * HDIM, (head + 1) * HDIM)
                scores = dot_nn(kh_ref[head, rows, :], queries)
                probs = jnp.exp(scores - lse_ref[head:head + 1, columns])
                grad_weights = dot_nn(vh_ref[head, rows, :], grads)
                grad_scores = (probs * (grad_weights - delta_ref[head:head + 1, columns])).astype(BF16)
                dv_ref[part, :] += dot_nt(grads[part, :], probs.astype(BF16))
                dk_ref[part, :] += dot_nt(queries[part, :], grad_scores)
                dq_ref[part, columns] += dot_nn(kt_ref[part, rows], grad_scores)
            return 0

        lax.fori_loop(low, high, query_step, 0)
        out_ref[width:2 * width, rows] = dk_ref[...].astype(BF16)
        out_ref[2 * width:3 * width, rows] = dv_ref[...].astype(BF16)
        return 0

    lax.fori_loop(0, tiles, key_step, 0)
    out_ref[0:width, :] = (dq_ref[...] * (1.0 / math.sqrt(HDIM))).astype(BF16)


VM = pl.BlockSpec(memory_space=pltpu.VMEM)
SM = pl.BlockSpec(memory_space=pltpu.SMEM)
LIMIT = 60 * 2**20


def attn_fwd(lengths, tokens, gain, wq, wk, wv, blocks):
    group, model = tokens.shape
    width = wq.shape[0]
    lanes = wk.shape[0]
    heads = width // HDIM
    tiles = group // TILE
    S = jax.ShapeDtypeStruct
    return pl.pallas_call(
        fwd_kernel,
        out_shape=(S((group, model), BF16), S((blocks, width, group // blocks), BF16), S((8, group), F32),
                   S((lanes, group), BF16), S((width, group), BF16), S((group, lanes), BF16), S((group, lanes), BF16)),
        in_specs=[SM] + [VM] * 5, out_specs=(VM,) * 7,
        scratch_shapes=[pltpu.VMEM((heads, group, lanes), BF16), pltpu.VMEM((width, group), BF16),
                        pltpu.VMEM((tiles, heads, TILE, TILE), F32)],
        compiler_params=pltpu.CompilerParams(vmem_limit_bytes=LIMIT),
        cost_estimate=pl.CostEstimate(flops=8 * 10**9, bytes_accessed=10**7, transcendentals=4 * 10**6),
        name="attend_forward",
    )(lengths, tokens, gain, wq, wk, wv)


def attn_bwd(own, lengths, q, kt, kn, vn, lse, att, do):
    width, group = kt.shape
    lanes = kn.shape[1]
    heads = width // HDIM
    S = jax.ShapeDtypeStruct
    return pl.pallas_call(
        bwd_kernel,
        out_shape=S((3 * width, group), BF16),
        in_specs=[SM] * 2 + [VM] * 7, out_specs=VM,
        scratch_shapes=[pltpu.VMEM((heads, group, lanes), BF16), pltpu.VMEM((heads, group, width), BF16),
                        pltpu.VMEM((8, group), F32), pltpu.VMEM((width, group), F32),
                        pltpu.VMEM((width, TILE), F32), pltpu.VMEM((width, TILE), F32)],
        compiler_params=pltpu.CompilerParams(vmem_limit_bytes=LIMIT),
        cost_estimate=pl.CostEstimate(flops=16 * 10**9, bytes_accessed=10**7, transcendentals=4 * 10**6),
        name="attend_backward",
    )(own, lengths, q, kt, kn, vn, lse, att, do)


MESH = pl.DeviceIdType.MESH


def remote(source, target, send, recv, **device):
    return pltpu.make_async_remote_copy(
        src_ref=source, dst_ref=target, send_sem=send, recv_sem=recv,
        device_id=device, device_id_type=MESH)


def greet(n_wide, n_narrow):
    me, here = lax.axis_index("wide"), lax.axis_index("narrow")
    barrier = pltpu.get_barrier_semaphore()
    for step in range(1, n_wide):
        pl.semaphore_signal(barrier, inc=1, device_id={"wide": lax.rem(me + step, n_wide)}, device_id_type=MESH)
    for bits in range(1, n_narrow):
        pl.semaphore_signal(barrier, inc=1, device_id={"narrow": here ^ bits}, device_id_type=MESH)
    pl.semaphore_wait(barrier, n_wide - 1 + n_narrow - 1)


def tail_kernel(grad_ref, dense_ref, small_ref, grad_sum_ref, dense_sum_ref, small_sum_ref,
                pair_in, chip_out, chip_in, half_in, half_sum, slab_in, small_in, small_mid, small_all,
                pair_send, pair_recv, chip_send, chip_recv, half_send, half_recv, slab_send, slab_recv,
                give_send, give_recv, last_send, last_recv, near_send, near_recv, all_send, all_recv):
    chunks, half = dense_ref.shape[0], dense_ref.shape[1]
    n_wide, n_narrow = 2 * half, small_ref.shape[0]
    me, here = lax.axis_index("wide"), lax.axis_index("narrow")
    core, chip = here ^ 1, here ^ 2
    side, spot, partner = lax.rem(me, 2), me // 2, me ^ 1
    greet(n_wide, n_narrow)

    def ahead(step):
        return lax.rem(spot + step, half)

    def behind(step):
        return lax.rem(spot + half - step, half)

    halves = [remote(dense_ref.at[c, :, 1 - side], half_in.at[c], half_send.at[c], half_recv.at[c], wide=partner)
              for c in range(chunks)]
    pairs = [remote(grad_ref.at[here ^ (1 + 2 * i)], pair_in.at[i], pair_send.at[i], pair_recv.at[i], narrow=core)
             for i in range(2)]
    near = [remote(small_ref.at[here ^ bits], small_in.at[bits], near_send.at[bits], near_recv.at[bits],
                   narrow=here ^ bits) for bits in range(1, n_narrow)]
    slabs = [[remote(half_sum.at[c, ahead(step)], slab_in.at[c, step], slab_send.at[c, step], slab_recv.at[c, step],
                     wide=2 * ahead(step) + side) for step in range(1, half)] for c in range(chunks)]
    gives = [[remote(dense_sum_ref.at[c, spot, side], dense_sum_ref.at[c, spot, side], give_send.at[c, step],
                     give_recv.at[c, step], wide=2 * ahead(step) + side) for step in range(1, half)]
             for c in range(chunks)]
    lasts = [remote(dense_sum_ref.at[c, :, side], dense_sum_ref.at[c, :, side], last_send.at[c], last_recv.at[c],
                    wide=partner) for c in range(chunks)]
    for one in near + pairs + halves:
        one.start()

    total = small_ref[here]
    for bits in range(1, n_narrow):
        near[bits - 1].wait_recv()
        total = total + small_in[bits]
    small_mid[...] = total
    everyone = [remote(small_mid, small_all.at[step], all_send.at[step], all_recv.at[step],
                       wide=lax.rem(me + step, n_wide)) for step in range(1, n_wide)]
    for one in everyone:
        one.start()

    for one in pairs:
        one.wait_recv()
    chip_out[...] = (grad_ref[chip].astype(F32) + pair_in[1].astype(F32)).astype(BF16)
    across = remote(chip_out, chip_in, chip_send, chip_recv, narrow=chip)
    across.start()
    grad_sum_ref[...] = grad_ref[here].astype(F32) + pair_in[0].astype(F32)

    def to_owners(c):
        halves[c].wait_recv()
        half_sum[c] = (dense_ref[c, :, side].astype(F32) + half_in[c].astype(F32)).astype(BF16)
        for one in slabs[c]:
            one.start()

    def to_peers(c):
        part = half_sum[c, spot].astype(F32)
        for step in range(1, half):
            slabs[c][step - 1].wait_recv()
            part = part + slab_in[c, step].astype(F32)
        dense_sum_ref[c, spot, side] = part.astype(BF16)
        for one in gives[c]:
            one.start()

    def to_partner(c):
        for step in range(1, half):
            source = behind(step)
            remote(dense_sum_ref.at[c, source, side], dense_sum_ref.at[c, source, side], give_send.at[c, step],
                   give_recv.at[c, step], wide=2 * source + side).wait_recv()
        lasts[c].start()

    for turn in range(chunks + 3):
        for stage, act in ((0, to_owners), (1, to_peers), (3, to_partner)):
            if 0 <= turn - stage < chunks:
                act(turn - stage)

    across.wait_recv()
    grad_sum_ref[...] = grad_sum_ref[...] + chip_in[...].astype(F32)
    total = small_mid[...]
    for step in range(1, n_wide):
        everyone[step - 1].wait_recv()
        total = total + small_all[step]
    small_sum_ref[...] = total
    for c in range(chunks):
        remote(dense_sum_ref.at[c, :, 1 - side], dense_sum_ref.at[c, :, 1 - side], last_send.at[c], last_recv.at[c],
               wide=partner).wait_recv()
    for one in pairs + near + halves + everyone + [across] + lasts + sum(slabs, []) + sum(gives, []):
        one.wait_send()


def tail_sums(grad, dense, small, n_wide):
    n_narrow, half, rows = small.shape[0], n_wide // 2, dense.shape[0]
    chunks = next(c for c in (3, 2, 1) if rows % (16 * n_wide * c) == 0 or c == 1)
    dense = dense.reshape(chunks, half, 2, rows // (chunks * n_wide), -1)
    S, V, D = jax.ShapeDtypeStruct, pltpu.VMEM, pltpu.SemaphoreType.DMA
    one_side = (chunks, half) + dense.shape[3:]
    sems = lambda *shape: [D(shape)] * 2
    grad_sum, dense_sum, small_sum = pl.pallas_call(
        tail_kernel,
        out_shape=(S(grad.shape[1:], F32), S(dense.shape, BF16), S(small.shape[1:], F32)),
        in_specs=[VM] * 3, out_specs=(VM,) * 3,
        scratch_shapes=[V((2,) + grad.shape[1:], BF16), V(grad.shape[1:], BF16), V(grad.shape[1:], BF16),
                        V(one_side, BF16), V(one_side, BF16), V(one_side, BF16),
                        V(small.shape, F32), V(small.shape[1:], F32), V((n_wide,) + small.shape[1:], F32)]
        + sems(2) + [D, D] + sems(chunks) + sems(chunks, half) * 2 + sems(chunks) + sems(n_narrow) + sems(n_wide),
        compiler_params=pltpu.CompilerParams(collective_id=1, has_side_effects=True, vmem_limit_bytes=LIMIT),
        cost_estimate=pl.CostEstimate(flops=10**6, bytes_accessed=10**8, transcendentals=0),
        name="tail_sums",
    )(grad, dense, small)
    return grad_sum, dense_sum.reshape(rows, -1), small_sum


def matmul(left, right):
    return jnp.dot(left, right, preferred_element_type=F32)


def inner_rows(left, right):
    return lax.dot_general(left, right, (((0,), (0,)), ((), ())), preferred_element_type=F32)


def times_transposed(left, right):
    return lax.dot_general(left, right, (((1,), (1,)), ((), ())), preferred_element_type=F32)


def norm_rows(values):
    mean_row = jnp.mean(values, axis=-1, keepdims=True)
    centred = values - mean_row
    variance = jnp.mean(centred * centred, axis=-1, keepdims=True)
    root_inv = lax.rsqrt(variance + norm_eps)
    return (centred * root_inv, root_inv)


def norm_back(grad_scaled, normed, root_inv):
    first_mean = jnp.mean(grad_scaled, axis=-1, keepdims=True)
    second_mean = jnp.mean(grad_scaled * normed, axis=-1, keepdims=True)
    return root_inv * (grad_scaled - first_mean - normed * second_mean)


def gelu_parts(pre_act):
    normal_cdf = 0.5 * (1.0 + lax.erf(pre_act * 0.7071067811865476))
    density = jnp.exp(-0.5 * pre_act * pre_act) * 0.3989422804014327
    return (pre_act * normal_cdf, normal_cdf + pre_act * density)


def flip(value, bit):
    size = lax.axis_size("narrow")
    return lax.ppermute(value, "narrow", [(i, i ^ bit) for i in range(size)])


def swap_wide(rows, experts):
    shape = rows.shape
    return lax.all_to_all(
        rows.reshape(experts, -1, shape[1]), "wide", split_axis=0, concat_axis=0, tiled=True
    ).reshape(shape)


def swap_narrow(blocks):
    return lax.all_to_all(blocks, "narrow", split_axis=0, concat_axis=0, tiled=True)


def local(
    tokens,
    cotangent,
    lengths,
    routes,
    capacity_slots,
    first_gain,
    second_gain,
    query_weight,
    key_weight,
    value_weight,
    out_weight,
    router_weight,
    expert_in,
    expert_out,
):
    experts = lax.axis_size("wide")
    narrow = lax.axis_size("narrow")
    own_expert = lax.axis_index("wide")
    own_block = lax.axis_index("narrow")
    block_rows, model = cotangent.shape
    capacity = (42 * block_rows + 20 * experts - 1) // (20 * experts)
    slots = -(-capacity // 8) * 8
    width = query_weight.shape[1]

    in_here, out_here = expert_in[0], expert_out[0]
    out_there = flip(out_here, 2)
    out_near = jnp.stack([out_weight, flip(out_weight, 1), flip(out_weight, 2), flip(out_weight, 3)])
    out_full = jnp.concatenate([
        lax.dynamic_index_in_dim(out_near, own_block ^ block, 0, keepdims=False) for block in range(narrow)
    ])

    place = jnp.where(capacity_slots < capacity, routes * slots + capacity_slots, experts * slots)
    slot_ids = jnp.arange(experts * slots, dtype=jnp.int32)
    select = (
        (place[:, 0:1] == slot_ids[None, :]) | (place[:, 1:2] == slot_ids[None, :])
    ).astype(BF16)
    cot_rows = swap_wide(inner_rows(select, cotangent).astype(BF16), experts)

    query_t, key_t, value_t = query_weight.T, key_weight.T, value_weight.T
    lanes = -(-(width + lengths.shape[1]) // 128) * 128
    pad = ((0, lanes - width), (0, 0))
    attn_in, att, lse, q_keep, kt_keep, kn_keep, vn_keep = attn_fwd(
        lengths, tokens, first_gain[None], query_t, jnp.pad(key_t, pad), jnp.pad(value_t, pad), narrow
    )
    att, out_there, cot_rows, in_here = lax.optimization_barrier((att, out_there, cot_rows, in_here))
    in_there = flip(in_here, 2)
    out_parts = [out_here, flip(out_here, 1), out_there, flip(out_there, 1)]
    backs = [times_transposed(cot_rows, w_out).astype(BF16) for w_out in out_parts]
    *backs, in_there = lax.optimization_barrier((*backs, in_there))
    in_parts = [in_here, flip(in_here, 1), in_there, flip(in_there, 1)]
    att_own = swap_narrow(att).reshape(narrow * width, block_rows)
    own_tokens = lax.dynamic_slice_in_dim(tokens, own_block * block_rows, block_rows, 0).astype(F32)
    hidden_one = own_tokens + inner_rows(att_own, out_full)
    normed_two, root_two = norm_rows(hidden_one)
    moe_in = (normed_two * second_gain).astype(BF16)
    rows = swap_wide(inner_rows(select, moe_in).astype(BF16), experts)

    logits = matmul(rows, router_weight)
    logit_exp = jnp.exp(logits - jnp.max(logits, axis=1, keepdims=True))
    probs = logit_exp / jnp.sum(logit_exp, axis=1, keepdims=True)
    mine = (jnp.arange(experts, dtype=jnp.int32) == own_expert).astype(F32)[None, :]
    gate = jnp.sum(probs * mine, axis=1, keepdims=True)
    grad_gate = jnp.zeros_like(gate)
    act_parts, pre_grads = [], []
    for w_in, back in zip(in_parts, backs):
        activated, slope = gelu_parts(matmul(rows, w_in))
        act_low = activated.astype(BF16)
        act_parts.append(act_low)
        grad_gate = grad_gate + jnp.sum(act_low.astype(F32) * back.astype(F32), axis=1, keepdims=True)
        pre_grads.append((gate * back.astype(F32) * slope).astype(BF16))
    grad_logits = (grad_gate * probs * (mine - gate)).astype(BF16)
    grad_sum = times_transposed(grad_logits, router_weight)
    for pre_grad, w_in in zip(pre_grads, in_parts):
        grad_sum = grad_sum + times_transposed(pre_grad, w_in)
    grad_home = swap_wide(grad_sum.astype(BF16), experts)
    result = sum(matmul(act, w_out) for act, w_out in zip(act_parts, out_parts))
    result_home = swap_wide((gate * result).astype(BF16), experts)
    grad_result = (gate * cot_rows.astype(F32)).astype(BF16)
    router_part = inner_rows(rows, grad_logits)
    out_grads = [inner_rows(act, grad_result) for act in act_parts]
    in_grads = [inner_rows(rows, pre_grad) for pre_grad in pre_grads]

    def sum_narrow(parts):
        one, three = flip(parts[1].astype(BF16), 1), flip(parts[3].astype(BF16), 1)
        keep = parts[0] + one.astype(F32)
        send = (parts[2] + three.astype(F32)).astype(BF16)
        return keep, flip(send, 2)

    out_keep, out_add = sum_narrow(out_grads)
    in_keep, in_add = sum_narrow(in_grads)

    grad_moe_in = matmul(select, grad_home)
    mixed = hidden_one + matmul(select, result_home)
    block_output = mixed.astype(BF16)
    second_part = jnp.sum(grad_moe_in * normed_two, axis=0)
    grad_hidden = cotangent.astype(F32) + norm_back(grad_moe_in * second_gain, normed_two, root_two)
    grad_branch = grad_hidden.astype(BF16)
    grad_att = times_transposed(out_full, grad_branch).astype(BF16)
    grad_att = grad_att.reshape(narrow, width, block_rows)

    def heads_for(bits):
        return lax.dynamic_index_in_dim(grad_att, own_block ^ bits, 0, keepdims=False)

    grad_heads = jnp.stack([heads_for(0)] + [flip(heads_for(bits), bits) for bits in range(1, narrow)])
    out_part = matmul(att_own, grad_branch)
    part_keep, part_add = sum_narrow([
        lax.dynamic_index_in_dim(out_part.reshape(narrow, width, model), own_block ^ bits, 0, keepdims=False)
        for bits in range(narrow)
    ])

    grad_qkv = attn_bwd(own_block.reshape(1), lengths, q_keep, kt_keep, kn_keep, vn_keep, lse, att, grad_heads)
    grad_qkv, out_add, in_add, part_add = lax.optimization_barrier((grad_qkv, out_add, in_add, part_add))
    out_grad = (out_keep + out_add.astype(F32))[None]
    in_grad = (in_keep + in_add.astype(F32))[None]
    out_part = part_keep + part_add.astype(F32)
    qkv_t = jnp.concatenate([query_t, key_t, value_t], axis=0)
    grad_attn_in = inner_rows(grad_qkv, qkv_t).astype(BF16).reshape(narrow, block_rows, model)

    qkv_part = matmul(grad_qkv, attn_in)
    first_part = jnp.sum(qkv_part * qkv_t.astype(F32), axis=0) / first_gain
    small = jnp.concatenate([router_part, second_part[:, None], first_part[:, None]], axis=1).T
    rows_small, lanes_small = -(-small.shape[0] // 8) * 8, -(-width // 128) * 128
    small = small.reshape(-1, narrow, width).transpose(1, 0, 2)
    small = jnp.pad(small, ((0, 0), (0, rows_small - small.shape[1]), (0, lanes_small - width)))
    dense = jnp.concatenate([qkv_part.astype(BF16), out_part.astype(BF16)], axis=0)
    grad_rows_att, dense, small = tail_sums(grad_attn_in, dense, small, experts)
    query_grad, key_grad, value_grad, out_weight_grad = (
        dense[i * width:(i + 1) * width].astype(F32) for i in range(4)
    )
    own_normed, own_root = norm_rows(own_tokens)
    token_grad = grad_hidden + norm_back(grad_rows_att * first_gain, own_normed, own_root)

    return (
        block_output,
        token_grad,
        small[experts + 1, 0:width],
        small[experts, 0:width],
        query_grad.T,
        key_grad.T,
        value_grad.T,
        out_weight_grad,
        small[0:experts, 0:width].T,
        in_grad,
        out_grad,
    )


def solution(mesh):
    in_specs = (
        P("wide", None),
        P(("wide", "narrow"), None),
        P("wide", None),
        P(("wide", "narrow"), None),
        P(("wide", "narrow"), None),
        P(),
        P(),
        P(None, "narrow"),
        P(None, "narrow"),
        P(None, "narrow"),
        P("narrow", None),
        P(),
        P("wide", None, "narrow"),
        P("wide", "narrow", None),
    )
    out_specs = (
        P(("wide", "narrow"), None),
        P(("wide", "narrow"), None),
        P("narrow"),
        P("narrow"),
        P(None, "narrow"),
        P(None, "narrow"),
        P(None, "narrow"),
        P("narrow", None),
        P("narrow", None),
        P("wide", None, "narrow"),
        P("wide", "narrow", None),
    )
    return jax.shard_map(local, mesh=mesh, in_specs=in_specs, out_specs=out_specs, check_vma=False)
```
